32 devices in a mesh: box: 4 (over y, core), dir: 8 (over z, x).
Axes of the slice: x: 2, y: 2, z: 4, core: 2. Of those that a mesh axis runs over, the one named last changes fastest.
Arguments:
- child_rad: float32 [64, 2, 128, 256], P('box', None, 'dir'), may hold values from -6 to 6
- parent_incoming: float32 [16, 2, 256, 512], P('box', None, 'dir'), may hold values from -6 to 6
- theta_interp: float32 [256, 128], replicated, may hold values from -0.5 to 0.5
- phi_interp: float32 [256, 512], replicated, may hold values from -0.375 to 0.375
- child_ops: float32 [40, 2, 128, 256], P(None, None, 'dir'), may hold values from -2 to 2
- parent_ops: float32 [40, 2, 256, 512], P(None, None, 'dir'), may hold values from -2 to 2
- child_parent: int32 [64], P('box'), may hold values from 0 to 15, as said below
- child_octant: int32 [64], P('box'), may hold values from 0 to 7, as said below
- far_child_src: int32 [64, 16], P('box'), may hold values from 0 to 63, as said below
- far_child_op: int32 [64, 16], P('box'), may hold values from 0 to 39
- far_child_len: int32 [64], P('box'), may hold values from 1 to 16
- far_parent_src: int32 [16, 8], P('box'), may hold values from 0 to 15, as said below
- far_parent_op: int32 [16, 8], P('box'), may hold values from 0 to 39
- far_parent_len: int32 [16], P('box'), may hold values from 1 to 8
Outputs:
- child_local: float32 [64, 2, 128, 256], P('box', None, 'dir')
- parent_local: float32 [16, 2, 256, 512], P('box', None, 'dir')
- parent_rad: float32 [16, 2, 256, 512], P('box', None, 'dir')
The draws below stay inside these ranges and needn't reach their ends.
Inputs may be any that keep to these rules, and one draw needn't show every extreme that they name: child_parent never falls; the children of parents 4 q to 4 q + 3 are exactly children 16 q to 16 q + 15, every parent has 2 to 6 children. `child_octant`: children of one parent have distinct octants. far_child_src[c, k] differs from c, and far_child_src[c, k] // 16 differs from c // 16 by at most 1. far_parent_src[p, k] differs from p, and far_parent_src[p, k] // 4 differs from p // 4 by at most 1.
All inputs are finite; a program needn't handle non-finite values.
Results may differ from the reference program's by a relative error of at most 0.0003.
Values sent between devices are 32-bit elements; how exact they have to be, the bound alone decides.
A program may use at most 64 MiB of HBM per device.

```python
import math
import jax
import jax.numpy as jnp
from jax import lax

THC = 128
PHC = 256
THP = 256
PHP = 512
MF = 16
MFP = 8
NOPS = 40
PB_DEV = 4
CB_DEV = 16
NC = 64
NP = 16


def tree_parts(key):
    subkey = jax.random.fold_in(key, 7)
    first_key, second_key = jax.random.split(subkey)
    offsets = jax.random.randint(first_key, (NP // 2,), -2, 3).astype(jnp.int32)
    counts = jnp.stack([4 + offsets, 4 - offsets], axis=1).reshape(NP)
    ends = jnp.cumsum(counts).astype(jnp.int32)
    starts = ends - counts
    children = jnp.arange(NC, dtype=jnp.int32)
    parent = jnp.sum((ends[None, :] <= children[:, None]).astype(jnp.int32), axis=1).astype(jnp.int32)
    position = children - starts[parent]
    orders = jax.vmap(lambda single: jax.random.permutation(single, 8))(jax.random.split(second_key, NP))
    octant = orders[parent, position].astype(jnp.int32)
    return (parent, octant)


def far_lists(key, per_device, total_boxes, longest, salt_value):
    subkey = jax.random.fold_in(key, salt_value)
    keys = jax.random.split(subkey, 6)
    boxes = jnp.arange(total_boxes, dtype=jnp.int32)
    block_index = boxes // per_device
    block_total = total_boxes // per_device
    window_low = jnp.maximum(block_index - 1, 0) * per_device
    window_high = jnp.minimum(block_index + 2, block_total) * per_device
    window_span = window_high - window_low - 1
    raw_bits = jax.random.randint(keys[0], (total_boxes, longest), 0, 1 << 30)
    candidate = window_low[:, None] + raw_bits % window_span[:, None]
    source = (candidate + (candidate >= boxes[:, None]).astype(jnp.int32)).astype(jnp.int32)
    which_op = jax.random.randint(keys[1], (total_boxes, longest), 0, NOPS).astype(jnp.int32)
    heavy = jax.random.randint(keys[2], (block_total,), 0, 4) == 0
    light_len = 1 + jax.random.randint(keys[3], (total_boxes,), 0, 1 << 30) % max(longest // 4, 1)
    heavy_len = 1 + jax.random.randint(keys[4], (total_boxes,), 0, 1 << 30) % longest
    length = jnp.where(heavy[block_index], heavy_len, light_len)
    chosen_box = jax.random.randint(keys[5], (), 0, total_boxes)
    length = jnp.where(boxes == chosen_box, longest, length).astype(jnp.int32)
    return (source, which_op, length)


def draw_child_parent(key, part):
    return tree_parts(key)[0]


def draw_child_octant(key, part):
    return tree_parts(key)[1]


def draw_far_child_src(key, part):
    return far_lists(key, CB_DEV, NC, MF, 11)[0]


def draw_far_child_op(key, part):
    return far_lists(key, CB_DEV, NC, MF, 11)[1]


def draw_far_child_len(key, part):
    return far_lists(key, CB_DEV, NC, MF, 11)[2]


def draw_far_parent_src(key, part):
    return far_lists(key, PB_DEV, NP, MFP, 23)[0]


def draw_far_parent_op(key, part):
    return far_lists(key, PB_DEV, NP, MFP, 23)[1]


def draw_far_parent_len(key, part):
    return far_lists(key, PB_DEV, NP, MFP, 23)[2]


def shard_levels(own_key, extent, pieces, least, high):
    level = 1.0
    for axis_at, shards_of in pieces:
        heights = jax.random.uniform(jax.random.fold_in(jax.random.fold_in(own_key, 6), axis_at), (shards_of,), jnp.float32, least / len(pieces), high / len(pieces))
        level = level * jnp.repeat(jnp.exp(heights), extent[axis_at] // shards_of).reshape((-1,) + (1,) * (len(extent) - 1 - axis_at))
    return level


def noise(stream_key, extent, width, reach, pieces=(), kind=jnp.bfloat16):
    loudness = shard_levels(stream_key, extent, pieces, -0.22, 0.18) if pieces else 1.0
    array = jax.random.normal(stream_key, extent, jnp.float32) * width * loudness
    return jnp.minimum(jnp.maximum(array, -reach), reach).astype(kind)


def setup_inputs(seed: int = 0) -> dict:
    key_list = jax.random.split(jax.random.key(seed), 15)
    child_rad = noise(key_list[0], (NC, 2, THC, PHC), 1.0, 6.0, ((0, 4), (2, 8)), jnp.float32)
    parent_incoming = noise(key_list[1], (NP, 2, THP, PHP), 1.0, 6.0, ((0, 4), (2, 8)), jnp.float32)
    theta_interp = noise(key_list[2], (THP, THC), THC ** -0.5, 0.5, (), jnp.float32)
    phi_interp = noise(key_list[3], (PHC, PHP), PHC ** -0.5, 0.375, (), jnp.float32)
    child_ops = noise(key_list[4], (NOPS, 2, THC, PHC), 0.3, 2.0, ((2, 8),), jnp.float32)
    parent_ops = noise(key_list[5], (NOPS, 2, THP, PHP), 0.3, 2.0, ((2, 8),), jnp.float32)
    child_parent = draw_child_parent(jax.random.fold_in(key_list[14], 71), 0)
    child_octant = draw_child_octant(jax.random.fold_in(key_list[14], 71), 0)
    far_child_src = draw_far_child_src(jax.random.fold_in(key_list[14], 71), 0)
    far_child_op = draw_far_child_op(jax.random.fold_in(key_list[14], 71), 0)
    far_child_len = draw_far_child_len(jax.random.fold_in(key_list[14], 71), 0)
    far_parent_src = draw_far_parent_src(jax.random.fold_in(key_list[14], 71), 0)
    far_parent_op = draw_far_parent_op(jax.random.fold_in(key_list[14], 71), 0)
    far_parent_len = draw_far_parent_len(jax.random.fold_in(key_list[14], 71), 0)
    return {"child_rad": child_rad, "parent_incoming": parent_incoming, "theta_interp": theta_interp, "phi_interp": phi_interp, "child_ops": child_ops, "parent_ops": parent_ops, "child_parent": child_parent, "child_octant": child_octant, "far_child_src": far_child_src, "far_child_op": far_child_op, "far_child_len": far_child_len, "far_parent_src": far_parent_src, "far_parent_op": far_parent_op, "far_parent_len": far_parent_len}


phase_scale = 6.0
highest = lax.Precision.HIGHEST


def octant_signs(octant):
    first = 1.0 - 2.0 * (octant % 2).astype(jnp.float32)
    second = 1.0 - 2.0 * ((octant // 2) % 2).astype(jnp.float32)
    third = 1.0 - 2.0 * ((octant // 4) % 2).astype(jnp.float32)
    return first, second, third


def phase_parts(octant, row_start, row_count, total_rows, col_count):
    angle_rows = (row_start + jnp.arange(row_count)).astype(jnp.float32)
    theta = math.pi * (angle_rows + 0.5) / total_rows
    azimuth = 2.0 * math.pi * jnp.arange(col_count).astype(jnp.float32) / col_count
    sin_theta = jnp.sin(theta)[:, None]
    along_x = sin_theta * jnp.cos(azimuth)[None, :]
    along_y = sin_theta * jnp.sin(azimuth)[None, :]
    along_z = jnp.cos(theta)[:, None] + 0.0 * azimuth[None, :]
    first, second, third = octant_signs(octant)
    argument = phase_scale * (first[:, None, None] * along_x + second[:, None, None] * along_y + third[:, None, None] * along_z)
    return jnp.cos(argument), jnp.sin(argument)


def translate(patterns, operators, source, which_op, length):
    start = jnp.zeros((source.shape[0],) + patterns.shape[1:], jnp.float32)

    def advance(total, column):
        picked = patterns[source[:, column]]
        chosen = operators[which_op[:, column]]
        live = (column < length).astype(jnp.float32)[:, None, None]
        real_part = chosen[:, 0] * picked[:, 0] - chosen[:, 1] * picked[:, 1]
        imag_part = chosen[:, 0] * picked[:, 1] + chosen[:, 1] * picked[:, 0]
        return total + jnp.stack([live * real_part, live * imag_part], axis=1), None

    result, unused = lax.scan(advance, start, jnp.arange(source.shape[1]))
    return result


def reference(child_rad, parent_incoming, theta_interp, phi_interp, child_ops, parent_ops, child_parent, child_octant, far_child_src, far_child_op, far_child_len, far_parent_src, far_parent_op, far_parent_len):
    along_phi = jnp.einsum("nctf,fg->nctg", child_rad, phi_interp, precision=highest)
    interp = jnp.einsum("jt,nctg->ncjg", theta_interp, along_phi, precision=highest)
    cosine, sine = phase_parts(child_octant, 0, THP, THP, PHP)
    shifted = jnp.stack([cosine * interp[:, 0] - sine * interp[:, 1], sine * interp[:, 0] + cosine * interp[:, 1]], axis=1)
    member = (child_parent[None, :] == jnp.arange(NP)[:, None]).astype(jnp.float32)
    parent_rad = jnp.einsum("pn,ncjg->pcjg", member, shifted, precision=highest)
    parent_local = parent_incoming + translate(parent_rad, parent_ops, far_parent_src, far_parent_op, far_parent_len)
    gathered = parent_local[child_parent]
    unshift = jnp.stack([cosine * gathered[:, 0] + sine * gathered[:, 1], cosine * gathered[:, 1] - sine * gathered[:, 0]], axis=1)
    back_theta = jnp.einsum("jt,ncjg->nctg", theta_interp, unshift, precision=highest)
    anterp = jnp.einsum("nctg,fg->nctf", back_theta, phi_interp, precision=highest)
    child_local = translate(child_rad, child_ops, far_child_src, far_child_op, far_child_len) + anterp
    return child_local, parent_local, parent_rad
```

```python
import functools
import math

import jax
import jax.numpy as jnp
from jax import lax
from jax.experimental import pallas as pl
from jax.experimental.pallas import tpu as pltpu
from jax.sharding import PartitionSpec as P

phase_scale = 6.0
highest = lax.Precision.HIGHEST


def neighbours(array):
    size = lax.axis_size("box")
    up = [(i, i + 1) for i in range(size - 1)]
    down = [(i + 1, i) for i in range(size - 1)]
    return lax.ppermute(array, "box", up), lax.ppermute(array, "box", down)


def octant_signs(octant):
    first = 1.0 - 2.0 * (octant % 2).astype(jnp.float32)
    second = 1.0 - 2.0 * (octant // 2 % 2).astype(jnp.float32)
    third = 1.0 - 2.0 * (octant // 4 % 2).astype(jnp.float32)
    return (first, second, third)


def phase_block(octant, row_start, row_count, total_rows, col_start, col_count, total_cols):
    angle_rows = (row_start + jnp.arange(row_count, dtype=jnp.int32)).astype(jnp.float32)
    theta = math.pi * (angle_rows + 0.5) / total_rows
    angle_cols = (col_start + jnp.arange(col_count, dtype=jnp.int32)).astype(jnp.float32)
    azimuth = 2.0 * math.pi * angle_cols / total_cols
    sin_theta = jnp.sin(theta)[:, None]
    along_x = sin_theta * jnp.cos(azimuth)[None, :]
    along_y = sin_theta * jnp.sin(azimuth)[None, :]
    along_z = jnp.cos(theta)[:, None] + 0.0 * azimuth[None, :]
    first, second, third = octant_signs(octant)
    argument = phase_scale * (
        first[:, None, None] * along_x
        + second[:, None, None] * along_y
        + third[:, None, None] * along_z
    )
    return (jnp.cos(argument), jnp.sin(argument))


def exchange_body(count, matrix_ref, x_ref, *refs):
    if len(refs) == 7:
        extra_ref, out_ref, got, ready, landed, send_sem, recv_sem = refs
    else:
        out_ref, got, ready, landed, send_sem, recv_sem = refs
        extra_ref = None
    me = lax.axis_index("dir")
    planes, depth, width = got.shape[1:]
    rows = ready.shape[2]
    barrier = pltpu.get_barrier_semaphore()
    for step in range(1, count):
        pl.semaphore_signal(
            barrier,
            inc=1,
            device_id={"dir": lax.rem(me + step, count)},
            device_id_type=pl.DeviceIdType.MESH,
        )
    pl.semaphore_wait(barrier, count - 1)

    def push(source, target, leg):
        copies = []
        for step in range(1, count):
            peer = lax.rem(me + step, count)
            copy = pltpu.make_async_remote_copy(
                src_ref=source.at[peer],
                dst_ref=target.at[me],
                send_sem=send_sem.at[leg, step],
                recv_sem=recv_sem.at[leg, step],
                device_id={"dir": peer},
                device_id_type=pl.DeviceIdType.MESH,
            )
            copy.start()
            copies.append(copy)
        return copies

    def settle(target, leg):
        for step in range(1, count):
            origin = lax.rem(me + count - step, count)
            pltpu.make_async_remote_copy(
                src_ref=target.at[origin],
                dst_ref=target.at[origin],
                send_sem=send_sem.at[leg, step],
                recv_sem=recv_sem.at[leg, step],
                device_id={"dir": origin},
                device_id_type=pl.DeviceIdType.MESH,
            ).wait_recv()

    first = push(x_ref, got, 0)
    got[me] = x_ref[me]
    settle(got, 0)
    for plane in range(planes):
        product = jnp.dot(
            matrix_ref[...],
            got[:, plane].reshape(count * depth, width),
            precision=highest,
            preferred_element_type=jnp.float32,
        )
        ready[:, plane] = product.reshape(count, rows, width)
    second = push(ready, landed, 1)
    landed[me] = ready[me]
    settle(landed, 1)
    if extra_ref is None:
        out_ref[...] = landed[...]
    else:
        out_ref[...] = landed[...] + extra_ref[...]
    for copy in first + second:
        copy.wait_send()


def exchange(matrix, x, extra, which):
    count, planes, depth, width = x.shape
    rows = matrix.shape[0] // count
    operands = (matrix, x) if extra is None else (matrix, x, extra)
    return pl.pallas_call(
        functools.partial(exchange_body, count),
        out_shape=jax.ShapeDtypeStruct((count, planes, rows, width), jnp.float32),
        in_specs=[pl.BlockSpec(memory_space=pltpu.VMEM)] * len(operands),
        out_specs=pl.BlockSpec(memory_space=pltpu.VMEM),
        scratch_shapes=[
            pltpu.VMEM((count, planes, depth, width), jnp.float32),
            pltpu.VMEM((count, planes, rows, width), jnp.float32),
            pltpu.VMEM((count, planes, rows, width), jnp.float32),
            pltpu.SemaphoreType.DMA((2, count)),
            pltpu.SemaphoreType.DMA((2, count)),
        ],
        compiler_params=pltpu.CompilerParams(collective_id=which, has_side_effects=True),
        name="exchange_" + str(which),
    )(*operands)


def translate_body(has_base, *refs):
    source_ref, which_ref, length_ref, before, own, after, ops_ref = refs[:7]
    base_ref = refs[7] if has_base else None
    out_ref, wide, sems = refs[-3:]
    boxes, _, rows, width = own.shape
    copies = [
        pltpu.make_async_copy(part, wide.at[pl.ds(at * boxes, boxes)], sems.at[at])
        for at, part in enumerate((before, own, after))
    ]
    for copy in copies:
        copy.start()
    for copy in copies:
        copy.wait()
    offset = (lax.axis_index("box") - 1) * boxes
    tall = rows
    while tall % 16 == 0 and tall * width > 4096:
        tall //= 2

    def one_box(box, carry):
        length = length_ref[box]
        for start in range(0, rows, tall):
            part = slice(start, start + tall)

            def entry(column, totals):
                real, imag = totals
                at = source_ref[box, column] - offset
                op = which_ref[box, column]
                op_real, op_imag = ops_ref[op, 0, part], ops_ref[op, 1, part]
                re, im = wide[at, 0, part], wide[at, 1, part]
                real = real + (op_real * re - op_imag * im)
                imag = imag + (op_real * im + op_imag * re)
                return real, imag

            if has_base:
                initial = (base_ref[box, 0, part], base_ref[box, 1, part])
            else:
                initial = (jnp.zeros((tall, width), jnp.float32),) * 2
            real, imag = lax.fori_loop(0, length, entry, initial)
            out_ref[box, 0, part] = real
            out_ref[box, 1, part] = imag
        return carry

    lax.fori_loop(0, boxes, one_box, 0)


def translate(own, before, after, operators, source, which_op, length, base, name):
    boxes = own.shape[0]
    vmem = pl.BlockSpec(memory_space=pltpu.VMEM)
    smem = pl.BlockSpec(memory_space=pltpu.SMEM)
    anywhere = pl.BlockSpec(memory_space=pl.ANY)
    operands = [source, which_op, length, before, own, after, operators]
    specs = [smem] * 3 + [anywhere] * 3 + [vmem]
    if base is not None:
        operands.append(base)
        specs.append(vmem)
    return pl.pallas_call(
        functools.partial(translate_body, base is not None),
        out_shape=jax.ShapeDtypeStruct(own.shape, jnp.float32),
        in_specs=specs,
        out_specs=vmem,
        scratch_shapes=[
            pltpu.VMEM((3 * boxes,) + own.shape[1:], jnp.float32),
            pltpu.SemaphoreType.DMA((3,)),
        ],
        compiler_params=pltpu.CompilerParams(vmem_limit_bytes=40 * 1024 * 1024),
        name=name,
    )(*operands)


def per_device(
    child_rad,
    parent_incoming,
    theta_interp,
    phi_interp,
    child_ops,
    parent_ops,
    child_parent,
    child_octant,
    far_child_src,
    far_child_op,
    far_child_len,
    far_parent_src,
    far_parent_op,
    far_parent_len,
):
    child_count, _, theta_child, phi_child = child_rad.shape
    parent_count, _, theta_parent, phi_parent = parent_incoming.shape
    theta_total = theta_interp.shape[0]
    dir_count = lax.axis_size("dir")
    planes = child_count * 2 // dir_count
    padded = -(-theta_child // 8) * 8
    box_index = lax.axis_index("box")
    dir_index = lax.axis_index("dir")
    parent_slot = child_parent - box_index * parent_count
    member = (parent_slot[None, :] == jnp.arange(parent_count, dtype=jnp.int32)[:, None]).astype(
        jnp.float32
    )
    grow = ((0, 0), (0, 0), (0, padded - theta_child), (0, 0))
    spread = jnp.pad(
        theta_interp.reshape(theta_total, dir_count, theta_child),
        ((0, 0), (0, 0), (0, padded - theta_child)),
    ).reshape(theta_total, dir_count * padded)
    before, after = neighbours(child_rad)
    theta_done = exchange(
        spread, jnp.pad(child_rad, grow).reshape(dir_count, planes, padded, phi_child), None, 0
    )
    child_trans = translate(
        child_rad, before, after, child_ops, far_child_src, far_child_op, far_child_len, None,
        "child_translate",
    )
    theta_done = theta_done.reshape(child_count, 2, theta_parent, phi_child)
    interp = jnp.einsum("ncjf,fg->ncjg", theta_done, phi_interp, precision=highest)
    cosine, sine = phase_block(
        jnp.arange(8, dtype=jnp.int32), dir_index * theta_parent, theta_parent, theta_total,
        0, phi_parent, phi_parent,
    )
    cosine, sine = lax.optimization_barrier((cosine, sine))
    cosine, sine = cosine[child_octant], sine[child_octant]
    shifted = jnp.stack(
        [cosine * interp[:, 0] - sine * interp[:, 1], sine * interp[:, 0] + cosine * interp[:, 1]],
        axis=1,
    )
    parent_rad = jnp.einsum("pn,ncjg->pcjg", member, shifted, precision=highest)
    before, after = neighbours(parent_rad)
    parent_local = translate(
        parent_rad, before, after, parent_ops, far_parent_src, far_parent_op, far_parent_len,
        parent_incoming, "parent_translate",
    )
    own_field = parent_local[parent_slot]
    unshift = jnp.stack(
        [
            cosine * own_field[:, 0] + sine * own_field[:, 1],
            cosine * own_field[:, 1] - sine * own_field[:, 0],
        ],
        axis=1,
    )
    back_phi = jnp.einsum("ncjg,fg->ncjf", unshift, phi_interp, precision=highest)
    extra = jnp.pad(child_trans, grow).reshape(dir_count, planes, padded, phi_child)
    child_local = exchange(
        spread.T, back_phi.reshape(dir_count, planes, theta_parent, phi_child), extra, 1
    )
    child_local = child_local.reshape(child_count, 2, padded, phi_child)[:, :, :theta_child]
    return (child_local, parent_local, parent_rad)


def solution(mesh):
    in_specs = (
        P("box", None, "dir", None),
        P("box", None, "dir", None),
        P(),
        P(),
        P(None, None, "dir", None),
        P(None, None, "dir", None),
        P("box"),
        P("box"),
        P("box", None),
        P("box", None),
        P("box"),
        P("box", None),
        P("box", None),
        P("box"),
    )
    out_specs = (
        P("box", None, "dir", None),
        P("box", None, "dir", None),
        P("box", None, "dir", None),
    )
    return jax.shard_map(
        per_device, mesh=mesh, in_specs=in_specs, out_specs=out_specs, check_vma=False
    )
```

```python
import functools
import math

import jax
import jax.numpy as jnp
from jax import lax
from jax.experimental import pallas as pl
from jax.experimental.pallas import tpu as pltpu
from jax.sharding import PartitionSpec as P

phase_scale = 6.0
highest = lax.Precision.HIGHEST


def neighbours(array):
    size = lax.axis_size("box")
    up = [(i, i + 1) for i in range(size - 1)]
    down = [(i + 1, i) for i in range(size - 1)]
    return lax.ppermute(array, "box", up), lax.ppermute(array, "box", down)


def octant_signs(octant):
    first = 1.0 - 2.0 * (octant % 2).astype(jnp.float32)
    second = 1.0 - 2.0 * (octant // 2 % 2).astype(jnp.float32)
    third = 1.0 - 2.0 * (octant // 4 % 2).astype(jnp.float32)
    return (first, second, third)


def phase_block(octant, row_start, row_count, total_rows, col_start, col_count, total_cols):
    angle_rows = (row_start + jnp.arange(row_count, dtype=jnp.int32)).astype(jnp.float32)
    theta = math.pi * (angle_rows + 0.5) / total_rows
    angle_cols = (col_start + jnp.arange(col_count, dtype=jnp.int32)).astype(jnp.float32)
    azimuth = 2.0 * math.pi * angle_cols / total_cols
    sin_theta = jnp.sin(theta)[:, None]
    along_x = sin_theta * jnp.cos(azimuth)[None, :]
    along_y = sin_theta * jnp.sin(azimuth)[None, :]
    along_z = jnp.cos(theta)[:, None] + 0.0 * azimuth[None, :]
    first, second, third = octant_signs(octant)
    argument = phase_scale * (
        first[:, None, None] * along_x
        + second[:, None, None] * along_y
        + third[:, None, None] * along_z
    )
    return (jnp.cos(argument), jnp.sin(argument))


def flipped(index, mask):
    result = index
    bit = 1
    while bit <= mask:
        if mask & bit:
            result = result + bit - 2 * bit * lax.rem(lax.div(index, bit), 2)
        bit *= 2
    return result


def exchange_body(count, around, fields, matrix_ref, x_ref, *refs):
    refs = list(refs)
    extra_ref = None if around else refs.pop(0)
    out_ref = refs.pop(0)
    if around:
        below_ref, above_ref = refs.pop(0), refs.pop(0)
    got, ready, landed, send_sem, recv_sem = refs[:5]
    me = lax.axis_index("dir")
    planes, depth, width = got.shape[1:]
    rows = ready.shape[2]
    mesh_ids = pl.DeviceIdType.MESH
    barrier = pltpu.get_barrier_semaphore()
    steps = range(count - 1, 0, -1)

    def partner(step):
        if count & (count - 1):
            return lax.rem(me + step, count), lax.rem(me + count - step, count)
        peer = flipped(me, step)
        return peer, peer

    for step in steps:
        pl.semaphore_signal(
            barrier, inc=1, device_id={"dir": partner(step)[0]}, device_id_type=mesh_ids
        )
    greeted = count - 1
    if around:
        box = lax.axis_index("box")
        upper = lax.rem(box + 1, fields)
        lower = lax.rem(box + fields - 1, fields)
        for other in (upper, lower):
            pl.semaphore_signal(
                barrier, inc=1, device_id={"box": other}, device_id_type=mesh_ids
            )
        greeted += 2
    pl.semaphore_wait(barrier, greeted)

    def push(source, target, leg, plane):
        for step in steps:
            peer, _ = partner(step)
            copy = pltpu.make_async_remote_copy(
                src_ref=source.at[peer, plane],
                dst_ref=target.at[me, plane],
                send_sem=send_sem.at[leg, plane, step],
                recv_sem=recv_sem.at[leg, plane, step],
                device_id={"dir": peer},
                device_id_type=mesh_ids,
            )
            copy.start()
            started.append(copy)

    def settle(target, leg, plane):
        for step in steps:
            _, origin = partner(step)
            pltpu.make_async_remote_copy(
                src_ref=target.at[origin, plane],
                dst_ref=target.at[origin, plane],
                send_sem=send_sem.at[leg, plane, step],
                recv_sem=recv_sem.at[leg, plane, step],
                device_id={"dir": origin},
                device_id_type=mesh_ids,
            ).wait_recv()

    started = []
    for plane in range(planes):
        push(x_ref, got, 0, plane)
    ring = []
    if around:
        box_send, box_recv = refs[5:7]
        for at, (other, target) in enumerate(((upper, below_ref), (lower, above_ref))):
            copy = pltpu.make_async_remote_copy(
                src_ref=x_ref,
                dst_ref=target,
                send_sem=box_send.at[at],
                recv_sem=box_recv.at[at],
                device_id={"box": other},
                device_id_type=mesh_ids,
            )
            copy.start()
            ring.append(copy)
    got[me] = x_ref[me]
    for plane in range(planes):
        settle(got, 0, plane)
        product = jnp.dot(
            matrix_ref[...],
            got[:, plane].reshape(count * depth, width),
            precision=highest,
            preferred_element_type=jnp.float32,
        )
        ready[:, plane] = product.reshape(count, rows, width)
        push(ready, landed, 1, plane)
    landed[me] = ready[me]
    for plane in range(planes):
        settle(landed, 1, plane)
    if extra_ref is None:
        out_ref[...] = landed[...]
    else:
        out_ref[...] = landed[...].reshape(out_ref.shape) + extra_ref[...]
    for copy in started:
        copy.wait_send()
    for copy in ring:
        copy.wait()


def exchange(matrix, x, extra, which):
    count, planes, depth, width = x.shape
    rows = matrix.shape[0] // count
    around = extra is None
    operands = (matrix, x) if around else (matrix, x, extra)
    vmem = pl.BlockSpec(memory_space=pltpu.VMEM)
    result = jax.ShapeDtypeStruct(
        (count, planes, rows, width) if around else extra.shape, jnp.float32
    )
    ring = jax.ShapeDtypeStruct(x.shape, jnp.float32)
    scratch = [
        pltpu.VMEM((count, planes, depth, width), jnp.float32),
        pltpu.VMEM((count, planes, rows, width), jnp.float32),
        pltpu.VMEM((count, planes, rows, width), jnp.float32),
        pltpu.SemaphoreType.DMA((2, planes, count)),
        pltpu.SemaphoreType.DMA((2, planes, count)),
    ]
    if around:
        scratch += [pltpu.SemaphoreType.DMA((2,)), pltpu.SemaphoreType.DMA((2,))]
    return pl.pallas_call(
        functools.partial(exchange_body, count, around, lax.axis_size("box")),
        out_shape=(result, ring, ring) if around else result,
        in_specs=[vmem] * len(operands),
        out_specs=(vmem,) * 3 if around else vmem,
        scratch_shapes=scratch,
        compiler_params=pltpu.CompilerParams(collective_id=which, has_side_effects=True),
        name="exchange_" + str(which),
    )(*operands)


def translate_body(has_base, *refs):
    source_ref, which_ref, length_ref, before, own, after, ops_ref = refs[:7]
    base_ref = refs[7] if has_base else None
    out_ref, wide, sems = refs[-3:]
    boxes, _, rows, width = own.shape
    copies = [
        pltpu.make_async_copy(part, wide.at[pl.ds(at * boxes, boxes)], sems.at[at])
        for at, part in enumerate((before, own, after))
    ]
    for copy in copies:
        copy.start()
    for copy in copies:
        copy.wait()
    offset = (lax.axis_index("box") - 1) * boxes
    tall = rows
    while tall % 16 == 0 and tall * width > 4096:
        tall //= 2

    def one_box(box, carry):
        length = length_ref[box]
        for start in range(0, rows, tall):
            part = slice(start, start + tall)

            def entry(column, totals):
                real, imag = totals
                at = source_ref[box, column] - offset
                op = which_ref[box, column]
                op_real, op_imag = ops_ref[op, 0, part], ops_ref[op, 1, part]
                re, im = wide[at, 0, part], wide[at, 1, part]
                real = real + (op_real * re - op_imag * im)
                imag = imag + (op_real * im + op_imag * re)
                return real, imag

            if has_base:
                initial = (base_ref[box, 0, part], base_ref[box, 1, part])
            else:
                initial = (jnp.zeros((tall, width), jnp.float32),) * 2
            real, imag = lax.fori_loop(0, length, entry, initial)
            out_ref[box, 0, part] = real
            out_ref[box, 1, part] = imag
        return carry

    lax.fori_loop(0, boxes, one_box, 0)


def translate(own, before, after, operators, source, which_op, length, base, name):
    boxes = own.shape[0]
    vmem = pl.BlockSpec(memory_space=pltpu.VMEM)
    smem = pl.BlockSpec(memory_space=pltpu.SMEM)
    anywhere = pl.BlockSpec(memory_space=pl.ANY)
    operands = [source, which_op, length, before, own, after, operators]
    specs = [smem] * 3 + [anywhere] * 3 + [vmem]
    if base is not None:
        operands.append(base)
        specs.append(vmem)
    return pl.pallas_call(
        functools.partial(translate_body, base is not None),
        out_shape=jax.ShapeDtypeStruct(own.shape, jnp.float32),
        in_specs=specs,
        out_specs=vmem,
        scratch_shapes=[
            pltpu.VMEM((3 * boxes,) + own.shape[1:], jnp.float32),
            pltpu.SemaphoreType.DMA((3,)),
        ],
        compiler_params=pltpu.CompilerParams(vmem_limit_bytes=40 * 1024 * 1024),
        name=name,
    )(*operands)


def per_device(
    child_rad,
    parent_incoming,
    theta_interp,
    phi_interp,
    child_ops,
    parent_ops,
    child_parent,
    child_octant,
    far_child_src,
    far_child_op,
    far_child_len,
    far_parent_src,
    far_parent_op,
    far_parent_len,
):
    child_count, _, theta_child, phi_child = child_rad.shape
    parent_count, _, theta_parent, phi_parent = parent_incoming.shape
    theta_total = theta_interp.shape[0]
    dir_count = lax.axis_size("dir")
    planes = child_count * 2 // dir_count
    padded = -(-theta_child // 8) * 8
    box_index = lax.axis_index("box")
    dir_index = lax.axis_index("dir")
    parent_slot = child_parent - box_index * parent_count
    member = (parent_slot[None, :] == jnp.arange(parent_count, dtype=jnp.int32)[:, None]).astype(
        jnp.float32
    )
    grow = ((0, 0), (0, 0), (0, padded - theta_child), (0, 0))
    spread = jnp.pad(
        theta_interp.reshape(theta_total, dir_count, theta_child),
        ((0, 0), (0, 0), (0, padded - theta_child)),
    ).reshape(theta_total, dir_count * padded)
    grown = jnp.pad(child_rad, grow)
    theta_done, before, after = exchange(
        spread, grown.reshape(dir_count, planes, padded, phi_child), None, 0
    )
    before = before.reshape(grown.shape)[:, :, :theta_child]
    after = after.reshape(grown.shape)[:, :, :theta_child]
    child_trans = translate(
        child_rad, before, after, child_ops, far_child_src, far_child_op, far_child_len, None,
        "child_translate",
    )
    theta_done = theta_done.reshape(child_count, 2, theta_parent, phi_child)
    interp = jnp.einsum("ncjf,fg->ncjg", theta_done, phi_interp, precision=lax.Precision.HIGH)
    cosine, sine = phase_block(
        jnp.arange(8, dtype=jnp.int32), dir_index * theta_parent, theta_parent, theta_total,
        0, phi_parent, phi_parent,
    )
    cosine, sine = lax.optimization_barrier((cosine, sine))
    cosine, sine = cosine[child_octant], sine[child_octant]
    shifted = jnp.stack(
        [cosine * interp[:, 0] - sine * interp[:, 1], sine * interp[:, 0] + cosine * interp[:, 1]],
        axis=1,
    )
    parent_rad = jnp.einsum("pn,ncjg->pcjg", member, shifted, precision=highest)
    before, after = neighbours(parent_rad)
    parent_local = translate(
        parent_rad, before, after, parent_ops, far_parent_src, far_parent_op, far_parent_len,
        parent_incoming, "parent_translate",
    )
    own_field = parent_local[parent_slot]
    unshift = jnp.stack(
        [
            cosine * own_field[:, 0] + sine * own_field[:, 1],
            cosine * own_field[:, 1] - sine * own_field[:, 0],
        ],
        axis=1,
    )
    back_phi = jnp.einsum("ncjg,fg->ncjf", unshift, phi_interp, precision=lax.Precision.HIGH)
    extra = jnp.pad(child_trans, grow)
    child_local = exchange(
        spread.T, back_phi.reshape(dir_count, planes, theta_parent, phi_child), extra, 1
    )
    child_local = child_local[:, :, :theta_child]
    return (child_local, parent_local, parent_rad)


def solution(mesh):
    in_specs = (
        P("box", None, "dir", None),
        P("box", None, "dir", None),
        P(),
        P(),
        P(None, None, "dir", None),
        P(None, None, "dir", None),
        P("box"),
        P("box"),
        P("box", None),
        P("box", None),
        P("box"),
        P("box", None),
        P("box", None),
        P("box"),
    )
    out_specs = (
        P("box", None, "dir", None),
        P("box", None, "dir", None),
        P("box", None, "dir", None),
    )
    return jax.shard_map(
        per_device, mesh=mesh, in_specs=in_specs, out_specs=out_specs, check_vma=False
    )
```

```python
import functools
import math

import jax
import jax.numpy as jnp
from jax import lax
from jax.experimental import pallas as pl
from jax.experimental.pallas import tpu as pltpu
from jax.sharding import PartitionSpec as P

phase_scale = 6.0
highest = lax.Precision.HIGHEST


def neighbours(array):
    size = lax.axis_size("box")
    up = [(i, i + 1) for i in range(size - 1)]
    down = [(i + 1, i) for i in range(size - 1)]
    return lax.ppermute(array, "box", up), lax.ppermute(array, "box", down)


def octant_signs(octant):
    first = 1.0 - 2.0 * (octant % 2).astype(jnp.float32)
    second = 1.0 - 2.0 * (octant // 2 % 2).astype(jnp.float32)
    third = 1.0 - 2.0 * (octant // 4 % 2).astype(jnp.float32)
    return (first, second, third)


def phase_block(octant, row_start, row_count, total_rows, col_start, col_count, total_cols):
    angle_rows = (row_start + jnp.arange(row_count, dtype=jnp.int32)).astype(jnp.float32)
    theta = math.pi * (angle_rows + 0.5) / total_rows
    angle_cols = (col_start + jnp.arange(col_count, dtype=jnp.int32)).astype(jnp.float32)
    azimuth = 2.0 * math.pi * angle_cols / total_cols
    sin_theta = jnp.sin(theta)[:, None]
    along_x = sin_theta * jnp.cos(azimuth)[None, :]
    along_y = sin_theta * jnp.sin(azimuth)[None, :]
    along_z = jnp.cos(theta)[:, None] + 0.0 * azimuth[None, :]
    first, second, third = octant_signs(octant)
    argument = phase_scale * (
        first[:, None, None] * along_x
        + second[:, None, None] * along_y
        + third[:, None, None] * along_z
    )
    return (jnp.cos(argument), jnp.sin(argument))


def flipped(index, mask):
    result = index
    bit = 1
    while bit <= mask:
        if mask & bit:
            result = result + bit - 2 * bit * lax.rem(lax.div(index, bit), 2)
        bit *= 2
    return result


def exchange_body(count, around, fields, matrix_ref, x_ref, *refs):
    refs = list(refs)
    out_ref = refs.pop(0)
    if around:
        below_ref, above_ref = refs.pop(0), refs.pop(0)
    got, ready, landed, send_sem, recv_sem = refs[:5]
    me = lax.axis_index("dir")
    planes, depth, width = got.shape[1:]
    rows = ready.shape[2]
    mesh_ids = pl.DeviceIdType.MESH
    barrier = pltpu.get_barrier_semaphore()
    steps = range(count - 1, 0, -1)

    def partner(step):
        if count & (count - 1):
            return lax.rem(me + step, count), lax.rem(me + count - step, count)
        peer = flipped(me, step)
        return peer, peer

    for step in steps:
        pl.semaphore_signal(
            barrier, inc=1, device_id={"dir": partner(step)[0]}, device_id_type=mesh_ids
        )
    greeted = count - 1
    if around:
        box = lax.axis_index("box")
        upper = lax.rem(box + 1, fields)
        lower = lax.rem(box + fields - 1, fields)
        for other in (upper, lower):
            pl.semaphore_signal(
                barrier, inc=1, device_id={"box": other}, device_id_type=mesh_ids
            )
        greeted += 2
    pl.semaphore_wait(barrier, greeted)

    def push(source, target, leg, plane):
        for step in steps:
            peer, _ = partner(step)
            copy = pltpu.make_async_remote_copy(
                src_ref=source.at[peer, plane],
                dst_ref=target.at[me, plane],
                send_sem=send_sem.at[leg, plane, step],
                recv_sem=recv_sem.at[leg, plane, step],
                device_id={"dir": peer},
                device_id_type=mesh_ids,
            )
            copy.start()
            started.append(copy)

    def settle(target, leg, plane):
        for step in steps:
            _, origin = partner(step)
            pltpu.make_async_remote_copy(
                src_ref=target.at[origin, plane],
                dst_ref=target.at[origin, plane],
                send_sem=send_sem.at[leg, plane, step],
                recv_sem=recv_sem.at[leg, plane, step],
                device_id={"dir": origin},
                device_id_type=mesh_ids,
            ).wait_recv()

    started = []
    for plane in range(planes):
        push(x_ref, got, 0, plane)
    got[me] = x_ref[me]
    for plane in range(planes):
        settle(got, 0, plane)
        product = lax.dot_general(
            matrix_ref[...],
            got[:, plane].reshape(count * depth, width),
            (((1 if around else 0,), (0,)), ((), ())),
            precision=highest,
            preferred_element_type=jnp.float32,
        )
        ready[:, plane] = product.reshape(count, rows, width)
        push(ready, landed, 1, plane)
    ring = []
    if around:
        box_send, box_recv = refs[5:7]
        for at, (other, target) in enumerate(((upper, below_ref), (lower, above_ref))):
            copy = pltpu.make_async_remote_copy(
                src_ref=x_ref,
                dst_ref=target,
                send_sem=box_send.at[at],
                recv_sem=box_recv.at[at],
                device_id={"box": other},
                device_id_type=mesh_ids,
            )
            copy.start()
            ring.append(copy)
    landed[me] = ready[me]
    for plane in range(planes):
        settle(landed, 1, plane)
    out_ref[...] = landed[...].reshape(out_ref.shape)
    for copy in started:
        copy.wait_send()
    for copy in ring:
        copy.wait()


def exchange(matrix, x, around, which):
    count, planes, depth, width = x.shape
    rows = matrix.shape[0 if around else 1] // count
    operands = (matrix, x)
    vmem = pl.BlockSpec(memory_space=pltpu.VMEM)
    result = jax.ShapeDtypeStruct((count * planes, rows, width), jnp.float32)
    ring = jax.ShapeDtypeStruct(x.shape, jnp.float32)
    scratch = [
        pltpu.VMEM((count, planes, depth, width), jnp.float32),
        pltpu.VMEM((count, planes, rows, width), jnp.float32),
        pltpu.VMEM((count, planes, rows, width), jnp.float32),
        pltpu.SemaphoreType.DMA((2, planes, count)),
        pltpu.SemaphoreType.DMA((2, planes, count)),
    ]
    if around:
        scratch += [pltpu.SemaphoreType.DMA((2,)), pltpu.SemaphoreType.DMA((2,))]
    return pl.pallas_call(
        functools.partial(exchange_body, count, around, lax.axis_size("box")),
        out_shape=(result, ring, ring) if around else result,
        in_specs=[vmem] * len(operands),
        out_specs=(vmem,) * 3 if around else vmem,
        scratch_shapes=scratch,
        compiler_params=pltpu.CompilerParams(
            collective_id=which, has_side_effects=True, vmem_limit_bytes=16 * 1024 * 1024
        ),
        name="exchange_" + str(which),
    )(*operands)


def translate_body(has_base, *refs):
    source_ref, which_ref, length_ref, before, own, after, ops_ref = refs[:7]
    base_ref = refs[7] if has_base else None
    out_ref, wide, sems = refs[-3:]
    boxes, _, rows, width = own.shape
    copies = [
        pltpu.make_async_copy(part, wide.at[pl.ds(at * boxes, boxes)], sems.at[at])
        for at, part in enumerate((before, own, after))
    ]
    for copy in copies:
        copy.start()
    for copy in copies:
        copy.wait()
    offset = (lax.axis_index("box") - 1) * boxes
    tall = rows
    while tall % 16 == 0 and tall * width > 4096:
        tall //= 2

    def one_box(box, carry):
        length = length_ref[box]
        for start in range(0, rows, tall):
            part = slice(start, start + tall)

            def entry(column, totals):
                real, imag = totals
                at = source_ref[box, column] - offset
                op = which_ref[box, column]
                op_real, op_imag = ops_ref[op, 0, part], ops_ref[op, 1, part]
                re, im = wide[at, 0, part], wide[at, 1, part]
                real = real + (op_real * re - op_imag * im)
                imag = imag + (op_real * im + op_imag * re)
                return real, imag

            if has_base:
                initial = (base_ref[box, 0, part], base_ref[box, 1, part])
            else:
                initial = (jnp.zeros((tall, width), jnp.float32),) * 2
            real, imag = lax.fori_loop(0, length, entry, initial)
            out_ref[box, 0, part] = real
            out_ref[box, 1, part] = imag
        return carry

    lax.fori_loop(0, boxes, one_box, 0)


def translate(own, before, after, operators, source, which_op, length, base, name):
    boxes = own.shape[0]
    vmem = pl.BlockSpec(memory_space=pltpu.VMEM)
    smem = pl.BlockSpec(memory_space=pltpu.SMEM)
    anywhere = pl.BlockSpec(memory_space=pltpu.HBM)
    operands = [source, which_op, length, before, own, after, operators]
    specs = [smem] * 3 + [anywhere] * 3 + [vmem]
    if base is not None:
        operands.append(base)
        specs.append(vmem)
    return pl.pallas_call(
        functools.partial(translate_body, base is not None),
        out_shape=jax.ShapeDtypeStruct(own.shape, jnp.float32),
        in_specs=specs,
        out_specs=vmem,
        scratch_shapes=[
            pltpu.VMEM((3 * boxes,) + own.shape[1:], jnp.float32),
            pltpu.SemaphoreType.DMA((3,)),
        ],
        compiler_params=pltpu.CompilerParams(vmem_limit_bytes=20 * 1024 * 1024),
        name=name,
    )(*operands)


def shift_body(parent_ref, octant_ref, cosine_ref, sine_ref, interp_ref, out_ref):
    children = interp_ref.shape[0]
    offset = lax.axis_index("box") * out_ref.shape[0]
    out_ref[...] = jnp.zeros_like(out_ref)

    def one_child(child, carry):
        slot, octant = parent_ref[child] - offset, octant_ref[child]
        cosine, sine = cosine_ref[octant], sine_ref[octant]
        real, imag = interp_ref[child, 0], interp_ref[child, 1]
        out_ref[slot, 0] += cosine * real - sine * imag
        out_ref[slot, 1] += sine * real + cosine * imag
        return carry

    lax.fori_loop(0, children, one_child, 0)


def unshift_body(parent_ref, octant_ref, cosine_ref, sine_ref, field_ref, out_ref):
    children = out_ref.shape[0]
    offset = lax.axis_index("box") * field_ref.shape[0]

    def one_child(child, carry):
        slot, octant = parent_ref[child] - offset, octant_ref[child]
        cosine, sine = cosine_ref[octant], sine_ref[octant]
        real, imag = field_ref[slot, 0], field_ref[slot, 1]
        out_ref[child, 0] = cosine * real + sine * imag
        out_ref[child, 1] = cosine * imag - sine * real
        return carry

    lax.fori_loop(0, children, one_child, 0)


def by_child(body, parent, octant, cosine, sine, values, boxes, name):
    vmem = pl.BlockSpec(memory_space=pltpu.VMEM)
    smem = pl.BlockSpec(memory_space=pltpu.SMEM)
    return pl.pallas_call(
        body,
        out_shape=jax.ShapeDtypeStruct((boxes,) + values.shape[1:], jnp.float32),
        in_specs=[smem] * 2 + [vmem] * 3,
        out_specs=vmem,
        compiler_params=pltpu.CompilerParams(vmem_limit_bytes=16 * 1024 * 1024),
        name=name,
    )(parent, octant, cosine, sine, values)


def per_device(
    child_rad,
    parent_incoming,
    theta_interp,
    phi_interp,
    child_ops,
    parent_ops,
    child_parent,
    child_octant,
    far_child_src,
    far_child_op,
    far_child_len,
    far_parent_src,
    far_parent_op,
    far_parent_len,
):
    child_count, _, theta_child, phi_child = child_rad.shape
    parent_count, _, theta_parent, phi_parent = parent_incoming.shape
    theta_total = theta_interp.shape[0]
    dir_count = lax.axis_size("dir")
    planes = child_count * 2 // dir_count
    padded = -(-theta_child // 8) * 8
    dir_index = lax.axis_index("dir")
    grow = ((0, 0), (0, 0), (0, padded - theta_child), (0, 0))
    spread = jnp.pad(
        theta_interp.reshape(theta_total, dir_count, theta_child),
        ((0, 0), (0, 0), (0, padded - theta_child)),
    ).reshape(theta_total, dir_count * padded)
    grown = jnp.pad(child_rad, grow)
    theta_done, before, after = exchange(
        spread, grown.reshape(dir_count, planes, padded, phi_child), True, 0
    )
    before = before.reshape(grown.shape)[:, :, :theta_child]
    after = after.reshape(grown.shape)[:, :, :theta_child]
    child_trans = translate(
        child_rad, before, after, child_ops, far_child_src, far_child_op, far_child_len, None,
        "child_translate",
    )
    theta_done = theta_done.reshape(child_count, 2, theta_parent, phi_child)
    interp = jnp.einsum("ncjf,fg->ncjg", theta_done, phi_interp, precision=lax.Precision.HIGH)
    cosine, sine = phase_block(
        jnp.arange(8, dtype=jnp.int32), dir_index * theta_parent, theta_parent, theta_total,
        0, phi_parent, phi_parent,
    )
    parent_rad = by_child(
        shift_body, child_parent, child_octant, cosine, sine, interp, parent_count, "shift"
    )
    before, after = neighbours(parent_rad)
    parent_local = translate(
        parent_rad, before, after, parent_ops, far_parent_src, far_parent_op, far_parent_len,
        parent_incoming, "parent_translate",
    )
    unshift = by_child(
        unshift_body, child_parent, child_octant, cosine, sine, parent_local, child_count, "unshift"
    )
    back_phi = jnp.einsum("ncjg,fg->ncjf", unshift, phi_interp, precision=lax.Precision.HIGH)
    anterp = exchange(
        spread, back_phi.reshape(dir_count, planes, theta_parent, phi_child), False, 1
    )
    anterp = anterp.reshape(child_count, 2, padded, phi_child)[:, :, :theta_child]
    child_local = child_trans + anterp
    return (child_local, parent_local, parent_rad)


def solution(mesh):
    in_specs = (
        P("box", None, "dir", None),
        P("box", None, "dir", None),
        P(),
        P(),
        P(None, None, "dir", None),
        P(None, None, "dir", None),
        P("box"),
        P("box"),
        P("box", None),
        P("box", None),
        P("box"),
        P("box", None),
        P("box", None),
        P("box"),
    )
    out_specs = (
        P("box", None, "dir", None),
        P("box", None, "dir", None),
        P("box", None, "dir", None),
    )
    return jax.shard_map(
        per_device, mesh=mesh, in_specs=in_specs, out_specs=out_specs, check_vma=False
    )
```

```python
import functools
import math

import jax
import jax.numpy as jnp
from jax import lax
from jax.experimental import pallas as pl
from jax.experimental.pallas import tpu as pltpu
from jax.sharding import PartitionSpec as P

phase_scale = 6.0
highest = lax.Precision.HIGHEST


def neighbours(array):
    size = lax.axis_size("box")
    up = [(i, i + 1) for i in range(size - 1)]
    down = [(i + 1, i) for i in range(size - 1)]
    return lax.ppermute(array, "box", up), lax.ppermute(array, "box", down)


def octant_signs(octant):
    first = 1.0 - 2.0 * (octant % 2).astype(jnp.float32)
    second = 1.0 - 2.0 * (octant // 2 % 2).astype(jnp.float32)
    third = 1.0 - 2.0 * (octant // 4 % 2).astype(jnp.float32)
    return (first, second, third)


def phase_block(octant, row_start, row_count, total_rows, col_start, col_count, total_cols):
    angle_rows = (row_start + jnp.arange(row_count, dtype=jnp.int32)).astype(jnp.float32)
    theta = math.pi * (angle_rows + 0.5) / total_rows
    angle_cols = (col_start + jnp.arange(col_count, dtype=jnp.int32)).astype(jnp.float32)
    azimuth = 2.0 * math.pi * angle_cols / total_cols
    sin_theta = jnp.sin(theta)[:, None]
    along_x = sin_theta * jnp.cos(azimuth)[None, :]
    along_y = sin_theta * jnp.sin(azimuth)[None, :]
    along_z = jnp.cos(theta)[:, None] + 0.0 * azimuth[None, :]
    first, second, third = octant_signs(octant)
    argument = phase_scale * (
        first[:, None, None] * along_x
        + second[:, None, None] * along_y
        + third[:, None, None] * along_z
    )
    return (jnp.cos(argument), jnp.sin(argument))


def flipped(index, mask):
    result = index
    bit = 1
    while bit <= mask:
        if mask & bit:
            result = result + bit - 2 * bit * lax.rem(lax.div(index, bit), 2)
        bit *= 2
    return result


def exchange_body(count, around, fields, matrix_ref, x_ref, *refs):
    refs = list(refs)
    out_ref = refs.pop(0)
    if around:
        below_ref, above_ref = refs.pop(0), refs.pop(0)
    got, ready, landed, send_sem, recv_sem = refs[:5]
    me = lax.axis_index("dir")
    planes, depth, width = got.shape[1:]
    rows = ready.shape[2]
    mesh_ids = pl.DeviceIdType.MESH
    barrier = pltpu.get_barrier_semaphore()
    steps = range(count - 1, 0, -1)

    def partner(step):
        if count & (count - 1):
            return lax.rem(me + step, count), lax.rem(me + count - step, count)
        peer = flipped(me, step)
        return peer, peer

    for step in steps:
        pl.semaphore_signal(
            barrier, inc=1, device_id={"dir": partner(step)[0]}, device_id_type=mesh_ids
        )
    greeted = count - 1
    if around:
        box = lax.axis_index("box")
        upper = lax.rem(box + 1, fields)
        lower = lax.rem(box + fields - 1, fields)
        for other in (upper, lower):
            pl.semaphore_signal(
                barrier, inc=1, device_id={"box": other}, device_id_type=mesh_ids
            )
        greeted += 2
    pl.semaphore_wait(barrier, greeted)

    def push(source, target, leg, plane):
        for step in steps:
            peer, _ = partner(step)
            copy = pltpu.make_async_remote_copy(
                src_ref=source.at[peer, plane],
                dst_ref=target.at[me, plane],
                send_sem=send_sem.at[leg, plane, step],
                recv_sem=recv_sem.at[leg, plane, step],
                device_id={"dir": peer},
                device_id_type=mesh_ids,
            )
            copy.start()
            started.append(copy)

    def settle(target, leg, plane):
        for step in steps:
            _, origin = partner(step)
            pltpu.make_async_remote_copy(
                src_ref=target.at[origin, plane],
                dst_ref=target.at[origin, plane],
                send_sem=send_sem.at[leg, plane, step],
                recv_sem=recv_sem.at[leg, plane, step],
                device_id={"dir": origin},
                device_id_type=mesh_ids,
            ).wait_recv()

    started = []
    for plane in range(planes):
        push(x_ref, got, 0, plane)
    got[me] = x_ref[me]
    for plane in range(planes):
        settle(got, 0, plane)
        product = lax.dot_general(
            matrix_ref[...],
            got[:, plane].reshape(count * depth, width),
            (((1 if around else 0,), (0,)), ((), ())),
            precision=lax.Precision.HIGH,
            preferred_element_type=jnp.float32,
        )
        ready[:, plane] = product.reshape(count, rows, width)
        push(ready, landed, 1, plane)
    ring = []
    if around:
        box_send, box_recv = refs[5:7]
        for at, (other, target) in enumerate(((upper, below_ref), (lower, above_ref))):
            copy = pltpu.make_async_remote_copy(
                src_ref=x_ref,
                dst_ref=target,
                send_sem=box_send.at[at],
                recv_sem=box_recv.at[at],
                device_id={"box": other},
                device_id_type=mesh_ids,
            )
            copy.start()
            ring.append(copy)
    landed[me] = ready[me]
    for plane in range(planes):
        settle(landed, 1, plane)
    out_ref[...] = landed[...].reshape(out_ref.shape)
    for copy in started:
        copy.wait_send()
    for copy in ring:
        copy.wait()


def exchange(matrix, x, around, which):
    count, planes, depth, width = x.shape
    rows = matrix.shape[0 if around else 1] // count
    operands = (matrix, x)
    vmem = pl.BlockSpec(memory_space=pltpu.VMEM)
    result = jax.ShapeDtypeStruct((count * planes, rows, width), jnp.float32)
    ring = jax.ShapeDtypeStruct(x.shape, jnp.float32)
    scratch = [
        pltpu.VMEM((count, planes, depth, width), jnp.float32),
        pltpu.VMEM((count, planes, rows, width), jnp.float32),
        pltpu.VMEM((count, planes, rows, width), jnp.float32),
        pltpu.SemaphoreType.DMA((2, planes, count)),
        pltpu.SemaphoreType.DMA((2, planes, count)),
    ]
    if around:
        scratch += [pltpu.SemaphoreType.DMA((2,)), pltpu.SemaphoreType.DMA((2,))]
    return pl.pallas_call(
        functools.partial(exchange_body, count, around, lax.axis_size("box")),
        out_shape=(result, ring, ring) if around else result,
        in_specs=[vmem] * len(operands),
        out_specs=(vmem,) * 3 if around else vmem,
        scratch_shapes=scratch,
        compiler_params=pltpu.CompilerParams(
            collective_id=which, has_side_effects=True, vmem_limit_bytes=16 * 1024 * 1024
        ),
        name="exchange_" + str(which),
    )(*operands)


def translate_body(has_base, *refs):
    source_ref, which_ref, length_ref, before, own, after, ops_ref = refs[:7]
    base_ref = refs[7] if has_base else None
    out_ref, wide, sems = refs[-3:]
    boxes, _, rows, width = own.shape
    copies = [
        pltpu.make_async_copy(part, wide.at[pl.ds(at * boxes, boxes)], sems.at[at])
        for at, part in enumerate((before, own, after))
    ]
    for copy in copies:
        copy.start()
    for copy in copies:
        copy.wait()
    offset = (lax.axis_index("box") - 1) * boxes
    tall = rows
    while tall % 16 == 0 and tall * width > 4096:
        tall //= 2

    def one_box(box, carry):
        length = length_ref[box]
        for start in range(0, rows, tall):
            part = slice(start, start + tall)

            def entry(column, totals):
                real, imag = totals
                at = source_ref[box, column] - offset
                op = which_ref[box, column]
                op_real, op_imag = ops_ref[op, 0, part], ops_ref[op, 1, part]
                re, im = wide[at, 0, part], wide[at, 1, part]
                real = real + (op_real * re - op_imag * im)
                imag = imag + (op_real * im + op_imag * re)
                return real, imag

            if has_base:
                initial = (base_ref[box, 0, part], base_ref[box, 1, part])
            else:
                initial = (jnp.zeros((tall, width), jnp.float32),) * 2
            real, imag = lax.fori_loop(0, length, entry, initial)
            out_ref[box, 0, part] = real
            out_ref[box, 1, part] = imag
        return carry

    lax.fori_loop(0, boxes, one_box, 0)


def translate(own, before, after, operators, source, which_op, length, base, name):
    boxes = own.shape[0]
    vmem = pl.BlockSpec(memory_space=pltpu.VMEM)
    smem = pl.BlockSpec(memory_space=pltpu.SMEM)
    anywhere = pl.BlockSpec(memory_space=pltpu.HBM)
    operands = [source, which_op, length, before, own, after, operators]
    specs = [smem] * 3 + [anywhere] * 3 + [vmem]
    if base is not None:
        operands.append(base)
        specs.append(vmem)
    return pl.pallas_call(
        functools.partial(translate_body, base is not None),
        out_shape=jax.ShapeDtypeStruct(own.shape, jnp.float32),
        in_specs=specs,
        out_specs=vmem,
        scratch_shapes=[
            pltpu.VMEM((3 * boxes,) + own.shape[1:], jnp.float32),
            pltpu.SemaphoreType.DMA((3,)),
        ],
        compiler_params=pltpu.CompilerParams(vmem_limit_bytes=20 * 1024 * 1024),
        name=name,
    )(*operands)


def shift_body(parent_ref, octant_ref, cosine_ref, sine_ref, interp_ref, out_ref):
    children = interp_ref.shape[0]
    offset = lax.axis_index("box") * out_ref.shape[0]
    out_ref[...] = jnp.zeros_like(out_ref)

    def one_child(child, carry):
        slot, octant = parent_ref[child] - offset, octant_ref[child]
        mirrored = octant // 4
        held = octant + mirrored * (7 - 2 * octant)
        sign = (1 - 2 * mirrored).astype(jnp.float32)
        cosine, sine = cosine_ref[held], sign * sine_ref[held]
        real, imag = interp_ref[child, 0], interp_ref[child, 1]
        out_ref[slot, 0] += cosine * real - sine * imag
        out_ref[slot, 1] += sine * real + cosine * imag
        return carry

    lax.fori_loop(0, children, one_child, 0)


def unshift_body(parent_ref, octant_ref, cosine_ref, sine_ref, field_ref, out_ref):
    children = out_ref.shape[0]
    offset = lax.axis_index("box") * field_ref.shape[0]

    def one_child(child, carry):
        slot, octant = parent_ref[child] - offset, octant_ref[child]
        mirrored = octant // 4
        held = octant + mirrored * (7 - 2 * octant)
        sign = (1 - 2 * mirrored).astype(jnp.float32)
        cosine, sine = cosine_ref[held], sign * sine_ref[held]
        real, imag = field_ref[slot, 0], field_ref[slot, 1]
        out_ref[child, 0] = cosine * real + sine * imag
        out_ref[child, 1] = cosine * imag - sine * real
        return carry

    lax.fori_loop(0, children, one_child, 0)


def by_child(body, parent, octant, cosine, sine, values, boxes, name):
    vmem = pl.BlockSpec(memory_space=pltpu.VMEM)
    smem = pl.BlockSpec(memory_space=pltpu.SMEM)
    return pl.pallas_call(
        body,
        out_shape=jax.ShapeDtypeStruct((boxes,) + values.shape[1:], jnp.float32),
        in_specs=[smem] * 2 + [vmem] * 3,
        out_specs=vmem,
        compiler_params=pltpu.CompilerParams(vmem_limit_bytes=16 * 1024 * 1024),
        name=name,
    )(parent, octant, cosine, sine, values)


def per_device(
    child_rad,
    parent_incoming,
    theta_interp,
    phi_interp,
    child_ops,
    parent_ops,
    child_parent,
    child_octant,
    far_child_src,
    far_child_op,
    far_child_len,
    far_parent_src,
    far_parent_op,
    far_parent_len,
):
    child_count, _, theta_child, phi_child = child_rad.shape
    parent_count, _, theta_parent, phi_parent = parent_incoming.shape
    theta_total = theta_interp.shape[0]
    dir_count = lax.axis_size("dir")
    planes = child_count * 2 // dir_count
    padded = -(-theta_child // 8) * 8
    dir_index = lax.axis_index("dir")
    grow = ((0, 0), (0, 0), (0, padded - theta_child), (0, 0))
    spread = jnp.pad(
        theta_interp.reshape(theta_total, dir_count, theta_child),
        ((0, 0), (0, 0), (0, padded - theta_child)),
    ).reshape(theta_total, dir_count * padded)
    grown = jnp.pad(child_rad, grow)
    theta_done, before, after = exchange(
        spread, grown.reshape(dir_count, planes, padded, phi_child), True, 0
    )
    before = before.reshape(grown.shape)[:, :, :theta_child]
    after = after.reshape(grown.shape)[:, :, :theta_child]
    child_trans = translate(
        child_rad, before, after, child_ops, far_child_src, far_child_op, far_child_len, None,
        "child_translate",
    )
    theta_done = theta_done.reshape(child_count, 2, theta_parent, phi_child)
    interp = jnp.einsum("ncjf,fg->ncjg", theta_done, phi_interp, precision=lax.Precision.HIGH)
    cosine, sine = phase_block(
        jnp.arange(4, dtype=jnp.int32), dir_index * theta_parent, theta_parent, theta_total,
        0, phi_parent, phi_parent,
    )
    parent_rad = by_child(
        shift_body, child_parent, child_octant, cosine, sine, interp, parent_count, "shift"
    )
    before, after = neighbours(parent_rad)
    parent_local = translate(
        parent_rad, before, after, parent_ops, far_parent_src, far_parent_op, far_parent_len,
        parent_incoming, "parent_translate",
    )
    unshift = by_child(
        unshift_body, child_parent, child_octant, cosine, sine, parent_local, child_count, "unshift"
    )
    back_phi = jnp.einsum("ncjg,fg->ncjf", unshift, phi_interp, precision=lax.Precision.HIGH)
    anterp = exchange(
        spread, back_phi.reshape(dir_count, planes, theta_parent, phi_child), False, 1
    )
    anterp = anterp.reshape(child_count, 2, padded, phi_child)[:, :, :theta_child]
    child_local = child_trans + anterp
    return (child_local, parent_local, parent_rad)


def solution(mesh):
    in_specs = (
        P("box", None, "dir", None),
        P("box", None, "dir", None),
        P(),
        P(),
        P(None, None, "dir", None),
        P(None, None, "dir", None),
        P("box"),
        P("box"),
        P("box", None),
        P("box", None),
        P("box"),
        P("box", None),
        P("box", None),
        P("box"),
    )
    out_specs = (
        P("box", None, "dir", None),
        P("box", None, "dir", None),
        P("box", None, "dir", None),
    )
    return jax.shard_map(
        per_device, mesh=mesh, in_specs=in_specs, out_specs=out_specs, check_vma=False
    )
```
